128 devices in a mesh: energy: 32 (over z, y, core), seg: 4 (over x).
Axes of the slice: x: 4, y: 4, z: 4, core: 2. Of those that a mesh axis runs over, the one named last changes fastest.
Arguments:
- lesser: float32 [128, 8, 2, 256, 256], P('energy', 'seg'), may hold values from -6 to 6
- greater: float32 [128, 8, 2, 256, 256], P('energy', 'seg'), may hold values from -6 to 6
- coupling_low: float32 [128, 8, 2, 256, 256], P('energy', 'seg'), may hold values from -0.125 to 0.125
- coupling_up: float32 [128, 8, 2, 256, 256], P('energy', 'seg'), may hold values from -0.125 to 0.125
Outputs:
- polarization: float32 [128, 8, 2, 256, 256], P('energy', 'seg')
- lesser_full: float32 [128, 8, 2, 256, 256], P('energy', 'seg')
The draws below stay inside these ranges and needn't reach their ends.
All inputs are finite; a program needn't handle non-finite values.
Results may differ from the reference program's by a relative error of at most 0.0001.
Values sent between devices are 32-bit elements; how exact they have to be, the bound alone decides.
No kernel may reach another device: no remote copies, remote signals or barrier semaphores. Data moves between devices by JAX's collectives and lax.ppermute only.
A program may use at most 128 MiB of HBM per device.

```python
import math
import jax
import jax.numpy as jnp
from jax import lax

BLOCK = 256
ENERGIES = 128
SEGMENTS = 8


def block_scale(own_key, dims, cuts, smallest, largest):
    def one(axis_at, blocks):
        heights = jax.random.uniform(jax.random.fold_in(jax.random.fold_in(own_key, 6), axis_at), (blocks,), jnp.float32, smallest / len(cuts), largest / len(cuts))
        return jnp.repeat(jnp.exp(heights), dims[axis_at] // blocks).reshape((-1,) + (1,) * (len(dims) - axis_at - 1))

    loudness = one(*cuts[0])
    for cut in cuts[1:]:
        loudness = loudness * one(*cut)
    return loudness


def noise(key, shape, width, limit, pieces=(), kind=jnp.bfloat16):
    loudness = block_scale(key, shape, pieces, -0.22, 0.18) if pieces else 1.0
    drawn = jax.random.normal(key, shape, jnp.float32) * width * loudness
    return jnp.minimum(jnp.maximum(drawn, -limit), limit).astype(kind)


def setup_inputs(seed: int = 0) -> dict:
    splits = jax.random.split(jax.random.key(seed), 5)
    lesser = noise(splits[0], (ENERGIES, SEGMENTS, 2, BLOCK, BLOCK), 1.0, 6.0, ((0, 32), (1, 4)), jnp.float32)
    greater = noise(splits[1], (ENERGIES, SEGMENTS, 2, BLOCK, BLOCK), 1.0, 6.0, ((0, 32), (1, 4)), jnp.float32)
    coupling_low = noise(splits[2], (ENERGIES, SEGMENTS, 2, BLOCK, BLOCK), (8 * BLOCK) ** -0.5, 0.125, ((0, 32), (1, 4)), jnp.float32)
    coupling_up = noise(splits[3], (ENERGIES, SEGMENTS, 2, BLOCK, BLOCK), (8 * BLOCK) ** -0.5, 0.125, ((0, 32), (1, 4)), jnp.float32)
    return {"lesser": lesser, "greater": greater, "coupling_low": coupling_low, "coupling_up": coupling_up}


def complex_product(former, latter):

    def multiply(one_part, two_part):
        return jnp.einsum('eij,ejk->eik', one_part, two_part, precision=lax.Precision.HIGHEST)
    real_part = multiply(former[:, 0], latter[:, 0]) - multiply(former[:, 1], latter[:, 1])
    imag_part = multiply(former[:, 0], latter[:, 1]) + multiply(former[:, 1], latter[:, 0])
    return jnp.stack([real_part, imag_part], axis=1)

def correlate_segment(pair_rows):
    lesser_seg, greater_seg = pair_rows
    energies_all = lesser_seg.shape[0]
    lesser_cplx = lax.complex(lesser_seg[:, 0], lesser_seg[:, 1])
    greater_cplx = lax.complex(greater_seg[:, 0], greater_seg[:, 1])
    lesser_freq = jnp.fft.fft(lesser_cplx, n=2 * energies_all, axis=0)
    greater_freq = jnp.fft.fft(greater_cplx, n=2 * energies_all, axis=0)
    joined = jnp.fft.ifft(lesser_freq * jnp.conj(greater_freq), axis=0)[:energies_all]
    joined = joined * (1.0 / math.sqrt(energies_all))
    return jnp.stack([jnp.real(joined), jnp.imag(joined)], axis=1).astype(lesser_seg.dtype)

def reference(lesser, greater, coupling_low, coupling_up):
    energies_all = lesser.shape[0]
    count = lesser.shape[1]
    block_size = lesser.shape[-1]
    eye_block = jnp.eye(block_size, dtype=lesser.dtype)
    identity = jnp.broadcast_to(jnp.stack([eye_block, jnp.zeros_like(eye_block)]), (energies_all, 2, block_size, block_size))
    corner_low = coupling_low + identity[:, None]
    corner_up = coupling_up + identity[:, None]
    lefts = [identity]
    for segment in range(1, count):
        lefts.append(complex_product(corner_low[:, segment - 1], lefts[-1]))
    rights = [identity]
    for segment in range(count - 2, -1, -1):
        rights.insert(0, complex_product(corner_up[:, segment + 1], rights[0]))
    transfer = jnp.stack([complex_product(lefts[segment], rights[segment]) for segment in range(count)], axis=1)
    lesser_full = lesser + transfer
    greater_full = greater + jnp.stack([transfer[:, :, 0], -transfer[:, :, 1]], axis=2)
    polar = lax.map(correlate_segment, (jnp.swapaxes(lesser_full, 0, 1), jnp.swapaxes(greater_full, 0, 1)))
    return (jnp.swapaxes(polar, 0, 1), lesser_full)
```

```python
import math

import jax
import jax.numpy as jnp
from jax import lax
from jax.experimental import pallas as pl
from jax.experimental.pallas import tpu as pltpu
from jax.sharding import PartitionSpec as P

F32 = jnp.float32
BF16 = jnp.bfloat16
HALF = 2
COLS = 2
VMEM = 56 * 1024 * 1024


def params():
    return pltpu.CompilerParams(vmem_limit_bytes=VMEM)


def cost(flops, nbytes):
    return pl.CostEstimate(flops=flops, bytes_accessed=nbytes, transcendentals=0)


def split(x):
    high = x.astype(BF16)
    return high, (x - high.astype(F32)).astype(BF16)


def dot3(left, right):
    lh, ll = left
    rh, rl = right

    def dot(a, b):
        return jnp.dot(a, b, preferred_element_type=F32)

    return dot(lh, rh) + (dot(lh, rl) + dot(ll, rh))


def as_left(real, imag):
    rh, rl = split(real)
    ih, il = split(imag)

    def block(r, i):
        return jnp.concatenate(
            [jnp.concatenate([r, -i], axis=1), jnp.concatenate([i, r], axis=1)], axis=0
        )

    return block(rh, ih), block(rl, il)


def as_right(real, imag):
    return split(jnp.concatenate([real, imag], axis=0))


def complex_product(left, right):
    size = left[0].shape[0]
    out = dot3(as_left(*left), as_right(*right))
    return out[:size], out[size:]


def eye(size):
    rows = lax.broadcasted_iota(jnp.int32, (size, size), 0)
    cols = lax.broadcasted_iota(jnp.int32, (size, size), 1)
    return jnp.where(rows == cols, 1.0, 0.0).astype(F32)


def totals_kernel(pieces, place_ref, low_ref, up_ref, first_ref, second_ref, *piece_refs):
    size = low_ref.shape[-1]
    width = size // pieces
    one = eye(size)
    low = complex_product(
        (low_ref[0, 1, 0] + one, low_ref[0, 1, 1]), (low_ref[0, 0, 0] + one, low_ref[0, 0, 1])
    )
    up = complex_product(
        (up_ref[0, 0, 0] + one, up_ref[0, 0, 1]), (up_ref[0, 1, 0] + one, up_ref[0, 1, 1])
    )
    lower_half = place_ref[0] <= 1
    for part in range(2):
        first = jnp.where(lower_half, low[part], up[part])
        first_ref[part] = first
        second_ref[part] = jnp.where(lower_half, up[part], low[part])
        for n in range(pieces):
            piece_refs[n][part] = first[:, n * width : (n + 1) * width]


def totals(place, low, up, energy):
    size = low.shape[-1]
    block = pl.BlockSpec((1, 2, 2, size, size), lambda i, _: (energy, 0, 0, 0, 0))

    def out(width):
        return pl.BlockSpec((2, size, width), lambda i, _: (0, 0, 0))

    widths = [size, size] + [size // COLS] * COLS
    return pl.pallas_call(
        lambda *refs: totals_kernel(COLS, *refs),
        out_shape=[jax.ShapeDtypeStruct((2, size, width), F32) for width in widths],
        grid_spec=pltpu.PrefetchScalarGridSpec(
            num_scalar_prefetch=1,
            grid=(1,),
            in_specs=[block, block],
            out_specs=[out(width) for width in widths],
        ),
        compiler_params=params(),
        cost_estimate=cost(6 * 16 * size**3, 28 * size * size * 4),
        name="totals",
    )(place, low, up)


def step_kernel(own_ref, seen_ref, out_ref):
    real, imag = complex_product((own_ref[0], own_ref[1]), (seen_ref[0], seen_ref[1]))
    out_ref[0] = real
    out_ref[1] = imag


def chain_step(own, seen):
    size, width = seen.shape[-2:]
    return pl.pallas_call(
        step_kernel,
        out_shape=jax.ShapeDtypeStruct(seen.shape, F32),
        compiler_params=params(),
        cost_estimate=cost(24 * size * size * width, 4 * size * (size + width) * 4),
        name="chain_step",
    )(own, seen)


def join_kernel(place_ref, *refs):
    count = 3 * HALF * COLS
    hops = refs[:count]
    low_ref, up_ref, lesser_ref, greater_ref, transfer_ref = refs[count : count + 5]
    sends = (refs[count + 5 : count + 10], refs[count + 10 : count + 15])
    held = refs[count + 15]
    size = low_ref.shape[-1]
    lanes = size // 2
    one = eye(size)
    place, z, y, core = (place_ref[n] for n in range(4))
    for n in range(HALF):

        def seen(hop, part):
            at = (hop * HALF + n) * COLS
            return jnp.concatenate([hops[at + piece][part] for piece in range(COLS)], axis=1)

        carried = []
        for at in (place, 3 - place):
            pair = []
            for part in range(2):
                value = one if part == 0 else jnp.zeros_like(one)
                for hop in range(3):
                    value = jnp.where(at == hop + 1, seen(hop, part), value)
                pair.append(value)
            carried.append(tuple(pair))
        prefix, suffix = carried
        low = (low_ref[n, 0] + one, low_ref[n, 1])
        up = (up_ref[n, 0] + one, up_ref[n, 1])
        terms = (
            complex_product(prefix, complex_product(up, suffix)),
            complex_product(complex_product(low, prefix), suffix),
        )
        for seg, (real, imag) in enumerate(terms):
            transfer_ref[n, seg, 0] = real
            transfer_ref[n, seg, 1] = imag
            held[0, n, seg, 0] = lesser_ref[n, seg, 0] + real
            held[0, n, seg, 1] = lesser_ref[n, seg, 1] + imag
            held[1, n, seg, 0] = greater_ref[n, seg, 0] + real
            held[1, n, seg, 1] = greater_ref[n, seg, 1] - imag

    for which in range(2):
        for lead in range(4):

            def copy(other, carry, which=which, lead=lead):
                to_z, to_y = (lead, other) if which == 0 else (other, lead)
                chip = lax.rem(z + to_z, 4) * 4 + lax.rem(y + to_y, 4)
                for to_core in range(2):
                    group = chip * 2 + lax.rem(core + to_core, 2)
                    rows = pl.ds(pl.multiple_of(group * 8, 8), 8)
                    for seg in range(2):
                        for n in range(HALF):
                            for part in range(2):
                                for side in range(2):
                                    cols = slice(side * lanes, (side + 1) * lanes)
                                    value = held[which, n, seg, part, rows, cols]
                                    if to_core == 0:
                                        sends[which][lead][other, seg, n, part, side] = value
                                    else:
                                        sends[which][4][lead, other, seg, n, part, side] = value
                return carry

            lax.fori_loop(0, 4, copy, 0)


def join(place, hops, low, up, lesser, greater, half):
    size = low.shape[-1]

    def full(shape):
        zeros = (0,) * len(shape)
        return pl.BlockSpec(shape, lambda i, _: zeros)

    def corner(seg):
        return pl.BlockSpec((HALF, 1, 2, size, size), lambda i, _: (half, seg, 0, 0, 0))

    both = pl.BlockSpec((HALF, 2, 2, size, size), lambda i, _: (half, 0, 0, 0, 0))
    block = (2, HALF, 2, 2, 8, size // 2)
    shapes = [(HALF, 2, 2, size, size)] + 2 * (4 * [(4,) + block] + [(4, 4) + block])

    def kernel(place_ref, *refs):
        refs = list(refs)
        at = len(hops)
        for n in (at, at + 1):
            refs[n] = refs[n].at[:, 0]
        join_kernel(place_ref, *refs)

    return pl.pallas_call(
        kernel,
        out_shape=[jax.ShapeDtypeStruct(shape, F32) for shape in shapes],
        grid_spec=pltpu.PrefetchScalarGridSpec(
            num_scalar_prefetch=1,
            grid=(1,),
            in_specs=[full(hop.shape) for hop in hops] + [corner(0), corner(1), both, both],
            out_specs=[full(shape) for shape in shapes],
            scratch_shapes=[pltpu.VMEM((2, HALF, 2, 2, size, size), F32)],
        ),
        compiler_params=params(),
        cost_estimate=cost(HALF * 4 * 24 * size**3, HALF * 20 * size * size * 4),
        name="join",
    )(place, *hops, low, up, lesser, greater)


def correlate_kernel(to_ref, back_ref, *refs):
    lesser = refs[0:8]
    greater = refs[8:16]
    sends = (refs[16:21], refs[21:26])
    to_high, to_low, back_high, back_low = refs[26:30]
    to_high[...], to_low[...] = split(to_ref[...])
    back_high[...], back_low[...] = split(back_ref[...])
    count = to_ref.shape[0] // 2

    def row(r, carry):
        def gather(arrays, swapped):
            pieces = []
            for side in range(2):
                rows = pl.ds(side * 8 + r, 8, stride=16)
                tiles = []
                for half in range(2):
                    for y in range(4):
                        for z in range(4):
                            at, inner = (z, y) if swapped else (y, z)
                            tiles.append(arrays[half * 4 + at][inner, 0, rows, :])
                pieces.append(jnp.concatenate(tiles, axis=0))
            return jnp.concatenate(pieces, axis=1)

        to = (to_high[...], to_low[...])
        one = dot3(to, split(gather(lesser, False)))
        two = dot3(to, split(gather(greater, True)))
        one_re, one_im, two_re, two_im = one[:count], one[count:], two[:count], two[count:]
        spectrum = jnp.concatenate(
            [one_re * two_re + one_im * two_im, one_im * two_re - one_re * two_im], axis=0
        )
        out = dot3((back_high[...], back_low[...]), split(spectrum))
        rows = pl.ds(r, 8, stride=8)
        for z in range(4):
            for y in range(4):
                for core in range(2):
                    at = ((z * 4 + y) * 2 + core) * 8
                    for side in range(2):
                        lead, other = (z, y) if side == 0 else (y, z)
                        value = out[at : at + 8, side * 128 : (side + 1) * 128]
                        if core == 0:
                            sends[side][lead][other, rows, :] = value
                        else:
                            sends[side][4][lead, other, rows, :] = value
        return carry

    lax.fori_loop(0, 8, row, 0)


def correlate(to, back, lesser, greater, seg):
    arrays = [a.reshape(4, 2, -1, a.shape[-1]) for a in lesser + greater]
    rows, lanes = arrays[0].shape[2:]
    shapes = 2 * (4 * [(4, rows // 2, lanes)] + [(4, 4, rows // 2, lanes)])

    def full(shape):
        zeros = (0,) * len(shape)
        return pl.BlockSpec(shape, lambda i: zeros)

    block = pl.BlockSpec((4, 1, rows, lanes), lambda i: (0, seg, 0, 0))
    points = to.shape[0]
    return pl.pallas_call(
        correlate_kernel,
        out_shape=[jax.ShapeDtypeStruct(shape, F32) for shape in shapes],
        grid=(1,),
        in_specs=[full(to.shape), full(back.shape)] + [block] * 16,
        out_specs=[full(shape) for shape in shapes],
        scratch_shapes=[pltpu.VMEM(to.shape, BF16)] * 2 + [pltpu.VMEM(back.shape, BF16)] * 2,
        compiler_params=params(),
        cost_estimate=cost(3 * 6 * points * 256 * 2048, 6 * 1024 * 1024),
        name="correlate",
    )(to, back, *arrays)


def place_kernel(place_ref, *refs):
    one, two = refs[0:4], refs[4:8]
    out_ref = refs[-1]
    z, y, core = (place_ref[n] for n in (1, 2, 3))
    for lead in range(4):

        def copy(other, carry, lead=lead):
            for side, arrays in enumerate((one, two)):
                from_z, from_y = (other, lead) if side == 0 else (lead, other)
                chip = lax.rem(z + 4 - from_z, 4) * 4 + lax.rem(y + 4 - from_y, 4)
                for from_core in range(2):
                    group = chip * 2 + lax.rem(core + from_core, 2)
                    rows = pl.ds(pl.multiple_of(group * 8, 8), 8)
                    for n in range(4):
                        for part in range(2):
                            at = (n * 2 + part) * 8
                            out_ref[n, 0, part, rows, side * 128 : (side + 1) * 128] = arrays[lead][
                                other, from_core, at : at + 8, :
                            ]
            return carry

        lax.fori_loop(0, 4, copy, 0)


def put_in_place(place, arrays, seg, shape, before):
    def full(shape):
        zeros = (0,) * len(shape)
        return pl.BlockSpec(shape, lambda i, _: zeros)

    extra = [] if before is None else [before]
    return pl.pallas_call(
        place_kernel,
        out_shape=jax.ShapeDtypeStruct(shape, F32),
        grid_spec=pltpu.PrefetchScalarGridSpec(
            num_scalar_prefetch=1,
            grid=(1,),
            in_specs=[full(a.shape) for a in arrays] + [pl.BlockSpec(memory_space=pl.ANY)] * len(extra),
            out_specs=pl.BlockSpec((shape[0], 1) + shape[2:], lambda i, _: (0, seg, 0, 0, 0)),
        ),
        input_output_aliases={1 + len(arrays): 0} if extra else {},
        compiler_params=params(),
        cost_estimate=cost(0, 4 * 1024 * 1024),
        name="put_in_place",
    )(place, *arrays, *extra)


def shift(z, y, core):
    def index(a, b, c):
        return (a % 4 * 4 + b % 4) * 2 + c % 2

    return [
        (index(a, b, c), index(a + z, b + y, c + core))
        for a in range(4)
        for b in range(4)
        for c in range(2)
    ]


def exchange(keep, swap, z_first, core_dim):
    def moved(arrays, along_z):
        return [arrays[0]] + [
            lax.ppermute(arrays[n], "energy", shift(n, 0, 0) if along_z else shift(0, n, 0))
            for n in range(1, 4)
        ]

    other = lax.ppermute(swap, "energy", shift(0, 0, 1))
    lead = moved([jnp.stack([keep[n], other[n]], axis=core_dim) for n in range(4)], z_first)
    return moved([jnp.stack([lead[n][k] for n in range(4)]) for k in range(4)], not z_first)


def transforms(place, energies):
    z, y, core = place[1], place[2], place[3]
    points = 2 * energies
    steps = jnp.arange(4, dtype=jnp.int32)
    twos = jnp.arange(2, dtype=jnp.int32)

    def ids(sign):
        return (
            lax.rem(z + 4 + sign * steps, 4)[:, None, None] * 8
            + lax.rem(y + 4 + sign * steps, 4)[None, :, None] * 2
            + lax.rem(core + twos, 2)[None, None, :]
        )

    came = jnp.swapaxes(ids(-1), 0, 1)
    came = (4 * came[None, :, :, :, None] + 2 * twos[:, None, None, None, None] + twos).reshape(-1)
    goes = (4 * ids(1)[..., None] + steps).reshape(-1)
    frequency = jnp.arange(points, dtype=jnp.int32)

    def table(ids):
        angle = (ids[:, None] * frequency[None, :] % points).astype(F32) * (2.0 * math.pi / points)
        return jnp.cos(angle), jnp.sin(angle)

    cosine, sine = table(came)
    to = jnp.concatenate(
        [
            jnp.stack([cosine, sine], axis=1).reshape(points, points).T,
            jnp.stack([-sine, cosine], axis=1).reshape(points, points).T,
        ],
        axis=0,
    )
    cosine, sine = table(goes)
    back = jnp.concatenate(
        [
            jnp.stack([cosine, sine], axis=1).reshape(points, points),
            jnp.stack([-sine, cosine], axis=1).reshape(points, points),
        ],
        axis=1,
    )
    return to, back * (1.0 / (points * math.sqrt(energies)))


HOPS = ([(0, 1), (3, 2)], [(1, 2), (2, 1)], [(2, 3), (1, 0)])


def on_device(lesser, greater, coupling_low, coupling_up):
    here = lesser.shape[0]
    group = lax.axis_index("energy").astype(jnp.int32)
    place = jnp.stack(
        [
            lax.axis_index("seg").astype(jnp.int32),
            group // 8,
            group // 2 % 4,
            group % 2,
        ]
    )
    own = [totals(place, coupling_low, coupling_up, n) for n in range(here)]
    chunks = [(n, piece) for n in range(here) for piece in range(COLS)]
    seen = {}
    for step in range(len(chunks) + 2):
        for hop in range(3):
            if 0 <= step - hop < len(chunks):
                n, piece = chunks[step - hop]
                if hop == 0:
                    sent = own[n][2 + piece]
                else:
                    sent = chain_step(own[n][hop - 1], seen[hop - 1, n, piece])
                seen[hop, n, piece] = lax.ppermute(sent, "seg", HOPS[hop])
    transfers, lesser_rows, greater_rows = [], [], []
    for half in range(here // HALF):
        hops = [
            seen[hop, half * HALF + n, piece]
            for hop in range(3)
            for n in range(HALF)
            for piece in range(COLS)
        ]
        out = join(place, hops, coupling_low, coupling_up, lesser, greater, half)
        transfers.append(out[0])
        lesser_rows += exchange(out[1:5], out[5], True, 2)
        greater_rows += exchange(out[6:10], out[10], False, 2)
    to, back = transforms(place, 32 * here)
    polarization = None
    for seg in range(2):
        out = correlate(to, back, lesser_rows, greater_rows, seg)
        arrays = exchange(out[0:4], out[4], True, 1) + exchange(out[5:9], out[9], False, 1)
        polarization = put_in_place(place, arrays, seg, lesser.shape, polarization)
    return polarization, lesser + jnp.concatenate(transfers)


def solution(mesh):
    spec = P("energy", "seg", None, None, None)
    return jax.shard_map(
        on_device,
        mesh=mesh,
        in_specs=(spec,) * 4,
        out_specs=(spec, spec),
        check_vma=False,
    )
```
